32 devices in a mesh: gx: 2 (over y), gy: 4 (over z), gz: 4 (over x, core).
Axes of the slice: x: 2, y: 2, z: 4, core: 2. Of those that a mesh axis runs over, the one named last changes fastest.
Arguments:
- blocks: float32 [2, 4, 4, 8, 128, 128], P('gx', 'gy', 'gz'), as said below
- columns: int32 [2, 4, 4, 8], replicated, may hold values from -1 to 31, as said below
Outputs:
- purified: float32 [2, 4, 4, 8, 128, 128], P('gx', 'gy', 'gz')
The draws below stay inside these ranges and needn't reach their ends.
Inputs may be any that keep to these rules, and one draw needn't show every extreme that they name: columns[i, 0] is i itself; every other entry is -1 or the number of a cluster that differs from i by one along exactly one of the three dimensions, repeats allowed. `blocks`: a block in a slot whose column is -1 is zero.
All inputs are finite; a program needn't handle non-finite values.
Results may differ from the reference program's by a relative error of at most 0.0003.
Values sent between devices are 32-bit elements; how exact they have to be, the bound alone decides.
A program may use at most 64 MiB of HBM per device.

```python
import math
import jax
import jax.numpy as jnp
from jax import lax

B = 128
K = 8
PURIFY = 1
NX = 2
NY = 4
NZ = 4


def pattern(key):
    clusters = NX * NY * NZ
    cluster_ids = jnp.arange(clusters, dtype=jnp.int32)
    coord_x = cluster_ids // (NY * NZ)
    coord_y = cluster_ids // NZ % NY
    coord_z = cluster_ids % NZ
    heading = jax.random.randint(jax.random.fold_in(key, 11), (clusters, K - 1), 0, 6)
    heading = heading.at[0, 0].set(0)
    step_x = jnp.where(heading == 0, -1, jnp.where(heading == 1, 1, 0))
    step_y = jnp.where(heading == 2, -1, jnp.where(heading == 3, 1, 0))
    step_z = jnp.where(heading == 4, -1, jnp.where(heading == 5, 1, 0))
    near_x = coord_x[:, None] + step_x
    near_y = coord_y[:, None] + step_y
    near_z = coord_z[:, None] + step_z
    inside = (near_x >= 0) & (near_x < NX) & (near_y >= 0) & (near_y < NY) & (near_z >= 0) & (near_z < NZ)
    others = jnp.where(inside, (near_x * NY + near_y) * NZ + near_z, -1)
    joined = jnp.concatenate([cluster_ids[:, None], others], axis=1)
    return joined.astype(jnp.int32).reshape(NX, NY, NZ, K)


def draw_columns(key, part):
    return pattern(jax.random.fold_in(key, 5))


def draw_blocks(key, part):
    pattern_cols = pattern(jax.random.fold_in(key, 5))
    sigma = 0.45 / math.sqrt(K * B)
    shape_all = (NX, NY, NZ, K, B, B)
    noise = jax.random.normal(jax.random.fold_in(key, 21), shape_all, jnp.float32)
    diag_vals = jax.random.uniform(jax.random.fold_in(key, 22), (NX, NY, NZ, B), jnp.float32, 0.2, 0.8)
    values = noise * sigma
    identity = jnp.eye(B, dtype=jnp.float32)
    first_slot = (jnp.arange(K) == 0).astype(jnp.float32)[:, None, None]
    values = values + first_slot * (diag_vals[:, :, :, None, None, :] * identity)
    live = (pattern_cols >= 0)[..., None, None]
    return jnp.where(live, values, 0.0).astype(jnp.float32)


def setup_inputs(seed: int = 0) -> dict:
    keys = jax.random.split(jax.random.key(seed), 3)
    return {
        "blocks": draw_blocks(jax.random.fold_in(keys[2], 71), 0),
        "columns": draw_columns(jax.random.fold_in(keys[2], 71), 0),
    }


exact_mode = lax.Precision.HIGHEST


def purify_once(current, flat_cols):
    flat_blocks = current.reshape(-1, K, B, B)

    def one_row(packed):
        row_blocks, row_cols = packed
        safe_cols = jnp.maximum(row_cols, 0)
        far_rows = flat_blocks[safe_cols]
        far_cols = flat_cols[safe_cols]
        matches = (far_cols[:, :, None] == row_cols[None, None, :]) & (row_cols[None, None, :] >= 0) & (row_cols[:, None, None] >= 0)
        picked = jnp.einsum("tus,tuab->tsab", matches.astype(jnp.float32), far_rows, precision=exact_mode)
        square = jnp.einsum("tab,tsbc->sac", row_blocks, picked, precision=exact_mode)
        cubed = jnp.einsum("tab,tsbc->sac", square, picked, precision=exact_mode)
        return 3.0 * square - 2.0 * cubed

    return lax.map(one_row, (flat_blocks, flat_cols)).reshape(current.shape)


def reference(blocks, columns):
    flat_cols = columns.reshape(-1, K)
    current = blocks
    for sweep in range(PURIFY):
        current = purify_once(current, flat_cols)
    return current
```

```python
import functools

import jax
import jax.numpy as jnp
from jax import lax
from jax.experimental import pallas as pl
from jax.experimental.pallas import tpu as pltpu
from jax.sharding import PartitionSpec as P

MESH = pl.DeviceIdType.MESH
AXES = ("gx", "gy", "gz")


def directions(sizes):
    found = []
    for axis, size in enumerate(sizes):
        if size == 2:
            found.append((axis, 0))
        elif size > 2:
            found.extend([(axis, -1), (axis, 1)])
    return found


def split(value):
    head = value.astype(jnp.bfloat16)
    tail = (value - head.astype(jnp.float32)).astype(jnp.bfloat16)
    return jnp.concatenate([head, tail], axis=1)


def product(left, right):
    width = right.shape[1] // 2
    both = jnp.dot(left, jnp.concatenate([right, right], axis=0), preferred_element_type=jnp.float32)
    return both[:, :width] + both[:, width:]


def kernel(
    sizes, cols, blocks, out,
    own, far_diag, far_edge, edge, half, acc, res, shown,
    load_sem, send_d, recv_d, send_e, recv_e, store_sem,
):
    dirs = directions(sizes)
    count = len(dirs)
    kslots, block_size = own.shape[0], own.shape[1]
    where_am_i = [lax.axis_index(name) for name in AXES]
    strides = (sizes[1] * sizes[2], sizes[2], 1)
    me = sum(place * stride for place, stride in zip(where_am_i, strides))

    def opposite(d):
        axis, step = dirs[d]
        return dirs.index((axis, -step))

    def target(d):
        axis, step = dirs[d]
        place = where_am_i[axis]
        return (1 - place) if step == 0 else place + step

    def neighbour_id(d):
        axis, _ = dirs[d]
        return me + (target(d) - where_am_i[axis]) * strides[axis]

    def exists(d):
        axis, step = dirs[d]
        if step == 0:
            return None
        place = where_am_i[axis]
        return place > 0 if step < 0 else place < sizes[axis] - 1

    def if_exists(d, action):
        there = exists(d)
        if there is None:
            action()
        else:
            pl.when(there)(action)

    def send(d, src, dst, send_sem, recv_sem):
        return pltpu.make_async_remote_copy(
            src_ref=src,
            dst_ref=dst.at[opposite(d)],
            send_sem=send_sem.at[d],
            recv_sem=recv_sem.at[opposite(d)],
            device_id={AXES[dirs[d][0]]: target(d)},
            device_id_type=MESH,
        )

    def arrival(d, src, dst, send_sem, recv_sem):
        return pltpu.make_async_remote_copy(
            src_ref=src,
            dst_ref=dst.at[d],
            send_sem=send_sem.at[d],
            recv_sem=recv_sem.at[d],
            device_id={AXES[dirs[d][0]]: target(d)},
            device_id_type=MESH,
        )

    load = pltpu.make_async_copy(blocks, own, load_sem)
    load.start()
    barrier = pltpu.get_barrier_semaphore()
    for d in range(count):
        if_exists(
            d,
            lambda d=d: pl.semaphore_signal(
                barrier, inc=1, device_id={AXES[dirs[d][0]]: target(d)}, device_id_type=MESH
            ),
        )
    for d in range(count):
        there = exists(d)
        if there is not None:

            @pl.when(jnp.logical_not(there))
            def _(d=d):
                far_diag[d] = jnp.zeros((block_size, block_size), jnp.float32)
                far_edge[d] = jnp.zeros((block_size, block_size), jnp.float32)

    named = [cols[where_am_i[0], where_am_i[1], where_am_i[2], s] for s in range(kslots)]
    matches = [[named[s] == neighbour_id(d) for s in range(1, kslots)] for d in range(count)]
    load.wait()
    for d in range(count):
        total = jnp.where(matches[d][0], own[1], 0.0)
        for s in range(2, kslots):
            total = total + jnp.where(matches[d][s - 1], own[s], 0.0)
        edge[d] = total
    peers = jnp.int32(0)
    for d in range(count):
        there = exists(d)
        peers = peers + (1 if there is None else there.astype(jnp.int32))
    pl.semaphore_wait(barrier, peers)
    for d in range(count):
        if_exists(d, lambda d=d: send(d, edge.at[d], far_edge, send_e, recv_e).start())
    for d in range(count):
        if_exists(d, lambda d=d: send(d, own.at[0], far_diag, send_d, recv_d).start())

    half[0] = split(own[0])
    for d in range(count):
        half[1 + d] = split(edge[d])
    for d in range(count):
        acc[d] = product(half[0], half[1 + d])
    square = product(half[0], half[0])
    order = list(range(count))[::-1]
    for d in order:
        if_exists(d, lambda d=d: arrival(d, edge.at[d], far_edge, send_e, recv_e).wait_recv())
        arrived = split(far_edge[d])
        half[1 + count + d] = arrived
        square = square + product(half[1 + d], arrived)
    own_square = split(square)
    cubed = product(own_square, half[0])
    for d in range(count):
        res[1 + d] = product(own_square, half[1 + d])
    for d in order:
        if_exists(d, lambda d=d: arrival(d, own.at[0], far_diag, send_d, recv_d).wait_recv())
        arrived = split(far_diag[d])
        near = acc[d] + product(half[1 + d], arrived)
        repeats = sum(match.astype(jnp.int32) for match in matches[d]).astype(jnp.float32)
        weighted = split(near * repeats)
        res[1 + d] = 3.0 * near - 2.0 * (res[1 + d] + product(weighted, arrived))
        cubed = cubed + product(weighted, half[1 + count + d])
    res[0] = jnp.zeros((block_size, block_size), jnp.float32)
    shown[0] = 3.0 * square - 2.0 * cubed
    pltpu.make_async_copy(shown.at[0], out.at[0], store_sem.at[0]).start()
    for s in range(1, kslots):
        index = jnp.int32(0)
        for d in range(count):
            index = jnp.where(matches[d][s - 1], 1 + d, index)
        shown[s] = res[index]
        pltpu.make_async_copy(shown.at[s], out.at[s], store_sem.at[s]).start()
    for s in range(kslots):
        pltpu.make_async_copy(shown.at[s], out.at[s], store_sem.at[s]).wait()
    for d in range(count):
        if_exists(d, lambda d=d: send(d, edge.at[d], far_edge, send_e, recv_e).wait_send())
        if_exists(d, lambda d=d: send(d, own.at[0], far_diag, send_d, recv_d).wait_send())


def on_device(sizes, blocks, columns):
    kslots, block_size = blocks.shape[3], blocks.shape[4]
    count = len(directions(sizes))
    block = (block_size, block_size)
    renewed = pl.pallas_call(
        functools.partial(kernel, sizes),
        out_shape=jax.ShapeDtypeStruct((kslots,) + block, jnp.float32),
        in_specs=[
            pl.BlockSpec(memory_space=pltpu.SMEM),
            pl.BlockSpec(memory_space=pl.ANY),
        ],
        out_specs=pl.BlockSpec(memory_space=pl.ANY),
        scratch_shapes=[
            pltpu.VMEM((kslots,) + block, jnp.float32),
            pltpu.VMEM((count,) + block, jnp.float32),
            pltpu.VMEM((count,) + block, jnp.float32),
            pltpu.VMEM((count,) + block, jnp.float32),
            pltpu.VMEM((1 + 2 * count, block_size, 2 * block_size), jnp.bfloat16),
            pltpu.VMEM((count,) + block, jnp.float32),
            pltpu.VMEM((1 + count,) + block, jnp.float32),
            pltpu.VMEM((kslots,) + block, jnp.float32),
            pltpu.SemaphoreType.DMA,
            pltpu.SemaphoreType.DMA((count,)),
            pltpu.SemaphoreType.DMA((count,)),
            pltpu.SemaphoreType.DMA((count,)),
            pltpu.SemaphoreType.DMA((count,)),
            pltpu.SemaphoreType.DMA((kslots,)),
        ],
        compiler_params=pltpu.CompilerParams(
            collective_id=0, has_side_effects=True, vmem_limit_bytes=8 * 1024 * 1024
        ),
    )(columns, blocks.reshape((kslots,) + block))
    return renewed.reshape(blocks.shape)


def solution(mesh):
    sizes = tuple(mesh.shape[name] for name in AXES)
    return jax.shard_map(
        functools.partial(on_device, sizes),
        mesh=mesh,
        in_specs=(P("gx", "gy", "gz", None, None, None), P()),
        out_specs=P("gx", "gy", "gz", None, None, None),
        check_vma=False,
    )
```

```python
import functools

import jax
import jax.numpy as jnp
from jax import lax
from jax.experimental import pallas as pl
from jax.experimental.pallas import tpu as pltpu
from jax.sharding import PartitionSpec as P

MESH = pl.DeviceIdType.MESH
AXES = ("gx", "gy", "gz")


def directions(sizes):
    found = []
    for axis, size in enumerate(sizes):
        if size == 2:
            found.append((axis, 0))
        elif size > 2:
            found.extend([(axis, -1), (axis, 1)])
    return found


def split(value):
    head = value.astype(jnp.bfloat16)
    tail = (value - head.astype(jnp.float32)).astype(jnp.bfloat16)
    return jnp.concatenate([head, tail], axis=1)


def product(left, right):
    width = right.shape[1] // 2
    both = jnp.dot(left, jnp.concatenate([right, right], axis=0), preferred_element_type=jnp.float32)
    return both[:, :width] + both[:, width:]


def kernel(
    sizes, cols_there, blocks, out,
    cols, own, far_diag, far_edge, edge, half, acc, res,
    cols_sem, load_sem, send_d, recv_d, send_e, recv_e,
):
    dirs = directions(sizes)
    count = len(dirs)
    kslots, block_size = own.shape[0], own.shape[1]
    where_am_i = [lax.axis_index(name) for name in AXES]
    strides = (sizes[1] * sizes[2], sizes[2], 1)
    me = sum(place * stride for place, stride in zip(where_am_i, strides))

    def opposite(d):
        axis, step = dirs[d]
        return dirs.index((axis, -step))

    def target(d):
        axis, step = dirs[d]
        place = where_am_i[axis]
        return (1 - place) if step == 0 else place + step

    def neighbour_id(d):
        axis, _ = dirs[d]
        return me + (target(d) - where_am_i[axis]) * strides[axis]

    def exists(d):
        axis, step = dirs[d]
        if step == 0:
            return None
        place = where_am_i[axis]
        return place > 0 if step < 0 else place < sizes[axis] - 1

    def if_exists(d, action):
        there = exists(d)
        if there is None:
            action()
        else:
            pl.when(there)(action)

    def send(d, src, dst, send_sem, recv_sem):
        return pltpu.make_async_remote_copy(
            src_ref=src,
            dst_ref=dst.at[opposite(d)],
            send_sem=send_sem.at[d],
            recv_sem=recv_sem.at[opposite(d)],
            device_id={AXES[dirs[d][0]]: target(d)},
            device_id_type=MESH,
        )

    def arrival(d, src, dst, send_sem, recv_sem):
        return pltpu.make_async_remote_copy(
            src_ref=src,
            dst_ref=dst.at[d],
            send_sem=send_sem.at[d],
            recv_sem=recv_sem.at[d],
            device_id={AXES[dirs[d][0]]: target(d)},
            device_id_type=MESH,
        )

    barrier = pltpu.get_barrier_semaphore()
    for d in range(count):
        if_exists(
            d,
            lambda d=d: pl.semaphore_signal(
                barrier, inc=1, device_id={AXES[dirs[d][0]]: target(d)}, device_id_type=MESH
            ),
        )
    named_load = pltpu.make_async_copy(cols_there, cols, cols_sem)
    named_load.start()
    load = pltpu.make_async_copy(blocks, own, load_sem)
    load.start()
    for d in range(count):
        there = exists(d)
        if there is not None:

            @pl.when(jnp.logical_not(there))
            def _(d=d):
                far_diag[d] = jnp.zeros((block_size, block_size), jnp.float32)
                far_edge[d] = jnp.zeros((block_size, block_size), jnp.float32)

    named_load.wait()
    named = [cols[where_am_i[0], where_am_i[1], where_am_i[2], s] for s in range(kslots)]
    matches = [[named[s] == neighbour_id(d) for s in range(1, kslots)] for d in range(count)]
    load.wait()
    for d in range(count):
        total = jnp.where(matches[d][0], own[1], 0.0)
        for s in range(2, kslots):
            total = total + jnp.where(matches[d][s - 1], own[s], 0.0)
        edge[d] = total
    peers = jnp.int32(0)
    for d in range(count):
        there = exists(d)
        peers = peers + (1 if there is None else there.astype(jnp.int32))
    pl.semaphore_wait(barrier, peers)
    for d in range(count):
        if_exists(d, lambda d=d: send(d, edge.at[d], far_edge, send_e, recv_e).start())
    for d in range(count):
        if_exists(d, lambda d=d: send(d, own.at[0], far_diag, send_d, recv_d).start())

    half[0] = split(own[0])
    for d in range(count):
        half[1 + d] = split(edge[d])
    for d in range(count):
        acc[d] = product(half[0], half[1 + d])
    square = product(half[0], half[0])
    order = list(range(count))[::-1]
    for d in order:
        if_exists(d, lambda d=d: arrival(d, edge.at[d], far_edge, send_e, recv_e).wait_recv())
        arrived = split(far_edge[d])
        half[1 + count + d] = arrived
        square = square + product(half[1 + d], arrived)
    own_square = split(square)
    cubed = product(own_square, half[0])
    for d in range(count):
        res[1 + d] = product(own_square, half[1 + d])
    for d in order:
        if_exists(d, lambda d=d: arrival(d, own.at[0], far_diag, send_d, recv_d).wait_recv())
        arrived = split(far_diag[d])
        near = acc[d] + product(half[1 + d], arrived)
        repeats = sum(match.astype(jnp.int32) for match in matches[d]).astype(jnp.float32)
        weighted = split(near * repeats)
        res[1 + d] = 3.0 * near - 2.0 * (res[1 + d] + product(weighted, arrived))
        cubed = cubed + product(weighted, half[1 + count + d])
    res[0] = jnp.zeros((block_size, block_size), jnp.float32)
    out[0] = 3.0 * square - 2.0 * cubed
    for s in range(1, kslots):
        index = jnp.int32(0)
        for d in range(count):
            index = jnp.where(matches[d][s - 1], 1 + d, index)
        out[s] = res[index]
    for d in range(count):
        if_exists(d, lambda d=d: send(d, edge.at[d], far_edge, send_e, recv_e).wait_send())
        if_exists(d, lambda d=d: send(d, own.at[0], far_diag, send_d, recv_d).wait_send())


def on_device(sizes, blocks, columns):
    kslots, block_size = blocks.shape[3], blocks.shape[4]
    count = len(directions(sizes))
    block = (block_size, block_size)
    renewed = pl.pallas_call(
        functools.partial(kernel, sizes),
        out_shape=pltpu.VMEM((kslots,) + block, jnp.float32),
        in_specs=[
            pl.BlockSpec(memory_space=pl.ANY),
            pl.BlockSpec(memory_space=pl.ANY),
        ],
        out_specs=pl.BlockSpec(memory_space=pltpu.VMEM),
        scratch_shapes=[
            pltpu.SMEM(columns.shape, jnp.int32),
            pltpu.VMEM((kslots,) + block, jnp.float32),
            pltpu.VMEM((count,) + block, jnp.float32),
            pltpu.VMEM((count,) + block, jnp.float32),
            pltpu.VMEM((count,) + block, jnp.float32),
            pltpu.VMEM((1 + 2 * count, block_size, 2 * block_size), jnp.bfloat16),
            pltpu.VMEM((count,) + block, jnp.float32),
            pltpu.VMEM((1 + count,) + block, jnp.float32),
            pltpu.SemaphoreType.DMA,
            pltpu.SemaphoreType.DMA,
            pltpu.SemaphoreType.DMA((count,)),
            pltpu.SemaphoreType.DMA((count,)),
            pltpu.SemaphoreType.DMA((count,)),
            pltpu.SemaphoreType.DMA((count,)),
        ],
        compiler_params=pltpu.CompilerParams(
            collective_id=0, has_side_effects=True
        ),
    )(columns, blocks.reshape((kslots,) + block))
    return renewed.reshape(blocks.shape)


def solution(mesh):
    sizes = tuple(mesh.shape[name] for name in AXES)
    return jax.shard_map(
        functools.partial(on_device, sizes),
        mesh=mesh,
        in_specs=(P("gx", "gy", "gz", None, None, None), P()),
        out_specs=P("gx", "gy", "gz", None, None, None),
        check_vma=False,
    )
```

```python
import functools

import jax
import jax.numpy as jnp
from jax import lax
from jax.experimental import pallas as pl
from jax.experimental.pallas import tpu as pltpu
from jax.sharding import PartitionSpec as P

MESH = pl.DeviceIdType.MESH
AXES = ("gx", "gy", "gz")


def directions(sizes):
    found = []
    for axis, size in enumerate(sizes):
        if size == 2:
            found.append((axis, 0))
        elif size > 2:
            found.extend([(axis, -1), (axis, 1)])
    return found


def split(value):
    head = value.astype(jnp.bfloat16)
    tail = (value - head.astype(jnp.float32)).astype(jnp.bfloat16)
    return jnp.concatenate([head, tail], axis=1)


def product(left, right):
    width = right.shape[1] // 2
    both = jnp.dot(left, jnp.concatenate([right, right], axis=0), preferred_element_type=jnp.float32)
    return both[:, :width] + both[:, width:]


def kernel(
    sizes, cols_there, blocks, out,
    cols, own, far_diag, far_edge, edge, half, acc, res,
    cols_sem, load_sem, send_d, recv_d, send_e, recv_e,
):
    dirs = directions(sizes)
    count = len(dirs)
    kslots, block_size = own.shape[0], own.shape[1]
    where_am_i = [lax.axis_index(name) for name in AXES]
    strides = (sizes[1] * sizes[2], sizes[2], 1)
    me = sum(place * stride for place, stride in zip(where_am_i, strides))

    def opposite(d):
        axis, step = dirs[d]
        return dirs.index((axis, -step))

    def target(d):
        axis, step = dirs[d]
        place = where_am_i[axis]
        return (1 - place) if step == 0 else place + step

    def neighbour_id(d):
        axis, _ = dirs[d]
        return me + (target(d) - where_am_i[axis]) * strides[axis]

    def exists(d):
        axis, step = dirs[d]
        if step == 0:
            return None
        place = where_am_i[axis]
        return place > 0 if step < 0 else place < sizes[axis] - 1

    def if_exists(d, action):
        there = exists(d)
        if there is None:
            action()
        else:
            pl.when(there)(action)

    def send(d, src, dst, send_sem, recv_sem):
        return pltpu.make_async_remote_copy(
            src_ref=src,
            dst_ref=dst.at[opposite(d)],
            send_sem=send_sem.at[d],
            recv_sem=recv_sem.at[opposite(d)],
            device_id={AXES[dirs[d][0]]: target(d)},
            device_id_type=MESH,
        )

    def arrival(d, src, dst, send_sem, recv_sem):
        return pltpu.make_async_remote_copy(
            src_ref=src,
            dst_ref=dst.at[d],
            send_sem=send_sem.at[d],
            recv_sem=recv_sem.at[d],
            device_id={AXES[dirs[d][0]]: target(d)},
            device_id_type=MESH,
        )

    barrier = pltpu.get_barrier_semaphore()
    for d in range(count):
        if_exists(
            d,
            lambda d=d: pl.semaphore_signal(
                barrier, inc=1, device_id={AXES[dirs[d][0]]: target(d)}, device_id_type=MESH
            ),
        )
    named_load = pltpu.make_async_copy(cols_there, cols, cols_sem)
    named_load.start()
    load = pltpu.make_async_copy(blocks, own, load_sem)
    load.start()
    for d in range(count):
        there = exists(d)
        if there is not None:

            @pl.when(jnp.logical_not(there))
            def _(d=d):
                far_diag[d] = jnp.zeros((block_size, block_size), jnp.float32)
                far_edge[d] = jnp.zeros((block_size, block_size), jnp.float32)

    named_load.wait()
    named = [cols[where_am_i[0], where_am_i[1], where_am_i[2], s] for s in range(kslots)]
    matches = [[named[s] == neighbour_id(d) for s in range(1, kslots)] for d in range(count)]
    load.wait()
    for d in range(count):
        total = jnp.where(matches[d][0], own[1], 0.0)
        for s in range(2, kslots):
            total = total + jnp.where(matches[d][s - 1], own[s], 0.0)
        edge[d] = total
    peers = jnp.int32(0)
    for d in range(count):
        there = exists(d)
        peers = peers + (1 if there is None else there.astype(jnp.int32))
    pl.semaphore_wait(barrier, peers)
    for d in range(count):
        if_exists(d, lambda d=d: send(d, edge.at[d], far_edge, send_e, recv_e).start())
    for d in range(count):
        if_exists(d, lambda d=d: send(d, own.at[0], far_diag, send_d, recv_d).start())

    half[0] = split(own[0])
    for d in range(count):
        half[1 + d] = split(edge[d])
    for d in range(count):
        acc[d] = product(half[0], half[1 + d])
    square = product(half[0], half[0])
    late = [d for d in range(count) if dirs[d][0] < 2]
    early = [d for d in range(count) if dirs[d][0] == 2]
    for group in (early, late):
        for d in group:
            if_exists(d, lambda d=d: arrival(d, edge.at[d], far_edge, send_e, recv_e).wait_recv())
    for d in range(count):
        half[1 + count + d] = split(far_edge[d])
        square = square + product(half[1 + d], half[1 + count + d])
    own_square = split(square)
    cubed = product(own_square, half[0])
    for d in range(count):
        res[1 + d] = product(own_square, half[1 + d])
    for group in (early, late):
        for d in group:
            if_exists(d, lambda d=d: arrival(d, own.at[0], far_diag, send_d, recv_d).wait_recv())
        arrived = {d: split(far_diag[d]) for d in group}
        near = {d: acc[d] + product(half[1 + d], arrived[d]) for d in group}
        for d in group:
            repeats = sum(match.astype(jnp.int32) for match in matches[d]).astype(jnp.float32)
            weighted = split(near[d] * repeats)
            res[1 + d] = 3.0 * near[d] - 2.0 * (res[1 + d] + product(weighted, arrived[d]))
            cubed = cubed + product(weighted, half[1 + count + d])
    res[0] = jnp.zeros((block_size, block_size), jnp.float32)
    out[0] = 3.0 * square - 2.0 * cubed
    for s in range(1, kslots):
        index = jnp.int32(0)
        for d in range(count):
            index = jnp.where(matches[d][s - 1], 1 + d, index)
        out[s] = res[index]
    for d in range(count):
        if_exists(d, lambda d=d: send(d, edge.at[d], far_edge, send_e, recv_e).wait_send())
        if_exists(d, lambda d=d: send(d, own.at[0], far_diag, send_d, recv_d).wait_send())


def on_device(sizes, blocks, columns):
    kslots, block_size = blocks.shape[3], blocks.shape[4]
    count = len(directions(sizes))
    block = (block_size, block_size)
    renewed = pl.pallas_call(
        functools.partial(kernel, sizes),
        out_shape=pltpu.VMEM((kslots,) + block, jnp.float32),
        in_specs=[
            pl.BlockSpec(memory_space=pl.ANY),
            pl.BlockSpec(memory_space=pl.ANY),
        ],
        out_specs=pl.BlockSpec(memory_space=pltpu.VMEM),
        scratch_shapes=[
            pltpu.SMEM(columns.shape, jnp.int32),
            pltpu.VMEM((kslots,) + block, jnp.float32),
            pltpu.VMEM((count,) + block, jnp.float32),
            pltpu.VMEM((count,) + block, jnp.float32),
            pltpu.VMEM((count,) + block, jnp.float32),
            pltpu.VMEM((1 + 2 * count, block_size, 2 * block_size), jnp.bfloat16),
            pltpu.VMEM((count,) + block, jnp.float32),
            pltpu.VMEM((1 + count,) + block, jnp.float32),
            pltpu.SemaphoreType.DMA,
            pltpu.SemaphoreType.DMA,
            pltpu.SemaphoreType.DMA((count,)),
            pltpu.SemaphoreType.DMA((count,)),
            pltpu.SemaphoreType.DMA((count,)),
            pltpu.SemaphoreType.DMA((count,)),
        ],
        compiler_params=pltpu.CompilerParams(
            collective_id=0, has_side_effects=True
        ),
    )(columns, blocks.reshape((kslots,) + block))
    return renewed.reshape(blocks.shape)


def solution(mesh):
    sizes = tuple(mesh.shape[name] for name in AXES)
    return jax.shard_map(
        functools.partial(on_device, sizes),
        mesh=mesh,
        in_specs=(P("gx", "gy", "gz", None, None, None), P()),
        out_specs=P("gx", "gy", "gz", None, None, None),
        check_vma=False,
    )
```

```python
import functools

import jax
import jax.numpy as jnp
from jax import lax
from jax.experimental import pallas as pl
from jax.experimental.pallas import tpu as pltpu
from jax.sharding import PartitionSpec as P

MESH = pl.DeviceIdType.MESH
AXES = ("gx", "gy", "gz")


def directions(sizes):
    found = []
    for axis, size in enumerate(sizes):
        if size == 2:
            found.append((axis, 0))
        elif size > 2:
            found.extend([(axis, -1), (axis, 1)])
    return found


def split(value):
    head = value.astype(jnp.bfloat16)
    tail = (value - head.astype(jnp.float32)).astype(jnp.bfloat16)
    return jnp.concatenate([head, tail], axis=1)


def product(left, right):
    width = right.shape[1] // 2
    both = jnp.dot(left, jnp.concatenate([right, right], axis=0), preferred_element_type=jnp.float32)
    return both[:, :width] + both[:, width:]


def kernel(
    sizes, cols_there, blocks, out,
    cols, own, far_diag, far_edge, edge, half, acc, res,
    cols_sem, load_sem, send_d, recv_d, send_e, recv_e, ready,
):
    dirs = directions(sizes)
    count = len(dirs)
    kslots, block_size = own.shape[0], own.shape[1]
    where_am_i = [lax.axis_index(name) for name in AXES]
    strides = (sizes[1] * sizes[2], sizes[2], 1)
    me = sum(place * stride for place, stride in zip(where_am_i, strides))

    def opposite(d):
        axis, step = dirs[d]
        return dirs.index((axis, -step))

    def target(d):
        axis, step = dirs[d]
        place = where_am_i[axis]
        return (1 - place) if step == 0 else place + step

    def neighbour_id(d):
        axis, _ = dirs[d]
        return me + (target(d) - where_am_i[axis]) * strides[axis]

    def exists(d):
        axis, step = dirs[d]
        if step == 0:
            return None
        place = where_am_i[axis]
        return place > 0 if step < 0 else place < sizes[axis] - 1

    def if_exists(d, action):
        there = exists(d)
        if there is None:
            action()
        else:
            pl.when(there)(action)

    def send(d, src, dst, send_sem, recv_sem):
        return pltpu.make_async_remote_copy(
            src_ref=src,
            dst_ref=dst.at[opposite(d)],
            send_sem=send_sem.at[d],
            recv_sem=recv_sem.at[opposite(d)],
            device_id={AXES[dirs[d][0]]: target(d)},
            device_id_type=MESH,
        )

    def arrival(d, src, dst, send_sem, recv_sem):
        return pltpu.make_async_remote_copy(
            src_ref=src,
            dst_ref=dst.at[d],
            send_sem=send_sem.at[d],
            recv_sem=recv_sem.at[d],
            device_id={AXES[dirs[d][0]]: target(d)},
            device_id_type=MESH,
        )

    def lower(d):
        axis, step = dirs[d]
        place = where_am_i[axis]
        return place > 0 if step < 0 else place == 1

    def upper(d):
        axis, step = dirs[d]
        place = where_am_i[axis]
        return place < sizes[axis] - 1 if step > 0 else place == 0

    lowers = [d for d in range(count) if dirs[d][1] <= 0]
    uppers = [d for d in range(count) if dirs[d][1] >= 0]

    def send_diag(d):
        return send(d, blocks.at[0], far_diag, send_d, recv_d)

    def send_edge(d):
        return send(d, edge.at[d], far_edge, send_e, recv_e)

    barrier = pltpu.get_barrier_semaphore()
    for d in uppers:

        @pl.when(upper(d))
        def _(d=d):
            pl.semaphore_signal(
                barrier, inc=1, device_id={AXES[dirs[d][0]]: target(d)}, device_id_type=MESH
            )

    named_load = pltpu.make_async_copy(cols_there, cols, cols_sem)
    named_load.start()
    load = pltpu.make_async_copy(blocks, own, load_sem)
    load.start()
    peers = jnp.int32(0)
    for d in lowers:
        peers = peers + lower(d).astype(jnp.int32)

    @pl.when(peers > 0)
    def _():
        pl.semaphore_wait(barrier, peers)

    for d in lowers:

        @pl.when(lower(d))
        def _(d=d):
            pl.semaphore_signal(
                ready.at[opposite(d)], inc=1, device_id={AXES[dirs[d][0]]: target(d)}, device_id_type=MESH
            )
            send_diag(d).start()

    for d in range(count):
        there = exists(d)
        if there is not None:

            @pl.when(jnp.logical_not(there))
            def _(d=d):
                far_diag[d] = jnp.zeros((block_size, block_size), jnp.float32)
                far_edge[d] = jnp.zeros((block_size, block_size), jnp.float32)

    named_load.wait()
    named = [cols[where_am_i[0], where_am_i[1], where_am_i[2], s] for s in range(kslots)]
    matches = [[named[s] == neighbour_id(d) for s in range(1, kslots)] for d in range(count)]
    load.wait()
    for d in range(count):
        total = jnp.where(matches[d][0], own[1], 0.0)
        for s in range(2, kslots):
            total = total + jnp.where(matches[d][s - 1], own[s], 0.0)
        edge[d] = total
    for d in lowers:
        pl.when(lower(d))(lambda d=d: send_edge(d).start())
    for d in uppers:

        @pl.when(upper(d))
        def _(d=d):
            pl.semaphore_wait(ready.at[d], 1)
            send_diag(d).start()
            send_edge(d).start()

    half[0] = split(own[0])
    for d in range(count):
        half[1 + d] = split(edge[d])
    for d in range(count):
        acc[d] = product(half[0], half[1 + d])
    square = product(half[0], half[0])
    late = [d for d in range(count) if dirs[d][0] < 2]
    early = [d for d in range(count) if dirs[d][0] == 2]
    for group in (early, late):
        for d in group:
            if_exists(d, lambda d=d: arrival(d, blocks.at[0], far_diag, send_d, recv_d).wait_recv())
        arrived = {d: split(far_diag[d]) for d in group}
        near = {d: acc[d] + product(half[1 + d], arrived[d]) for d in group}
        for d in group:
            repeats = sum(match.astype(jnp.int32) for match in matches[d]).astype(jnp.float32)
            weighted = split(near[d] * repeats)
            half[1 + count + d] = weighted
            acc[d] = 3.0 * near[d] - 2.0 * product(weighted, arrived[d])
    cubed = jnp.zeros((block_size, block_size), jnp.float32)
    for group in (early, late):
        for d in group:
            if_exists(d, lambda d=d: arrival(d, edge.at[d], far_edge, send_e, recv_e).wait_recv())
        for d in group:
            both = product(
                jnp.concatenate([half[1 + d], half[1 + count + d]], axis=0), split(far_edge[d])
            )
            square = square + both[:block_size]
            cubed = cubed + both[block_size:]
    own_square = split(square)
    for d in range(count):
        res[1 + d] = acc[d] - 2.0 * product(own_square, half[1 + d])
    cubed = cubed + product(own_square, half[0])
    res[0] = jnp.zeros((block_size, block_size), jnp.float32)
    out[0] = 3.0 * square - 2.0 * cubed
    for s in range(1, kslots):
        index = jnp.int32(0)
        for d in range(count):
            index = jnp.where(matches[d][s - 1], 1 + d, index)
        out[s] = res[index]
    for d in range(count):
        if_exists(d, lambda d=d: send_edge(d).wait_send())
        if_exists(d, lambda d=d: send_diag(d).wait_send())


def on_device(sizes, blocks, columns):
    kslots, block_size = blocks.shape[3], blocks.shape[4]
    count = len(directions(sizes))
    block = (block_size, block_size)
    renewed = pl.pallas_call(
        functools.partial(kernel, sizes),
        out_shape=pltpu.VMEM((kslots,) + block, jnp.float32),
        in_specs=[
            pl.BlockSpec(memory_space=pl.ANY),
            pl.BlockSpec(memory_space=pl.ANY),
        ],
        out_specs=pl.BlockSpec(memory_space=pltpu.VMEM),
        scratch_shapes=[
            pltpu.SMEM(columns.shape, jnp.int32),
            pltpu.VMEM((kslots,) + block, jnp.float32),
            pltpu.VMEM((count,) + block, jnp.float32),
            pltpu.VMEM((count,) + block, jnp.float32),
            pltpu.VMEM((count,) + block, jnp.float32),
            pltpu.VMEM((1 + 2 * count, block_size, 2 * block_size), jnp.bfloat16),
            pltpu.VMEM((count,) + block, jnp.float32),
            pltpu.VMEM((1 + count,) + block, jnp.float32),
            pltpu.SemaphoreType.DMA,
            pltpu.SemaphoreType.DMA,
            pltpu.SemaphoreType.DMA((count,)),
            pltpu.SemaphoreType.DMA((count,)),
            pltpu.SemaphoreType.DMA((count,)),
            pltpu.SemaphoreType.DMA((count,)),
            pltpu.SemaphoreType.REGULAR((count,)),
        ],
        compiler_params=pltpu.CompilerParams(
            collective_id=0, has_side_effects=True
        ),
    )(columns, blocks.reshape((kslots,) + block))
    return renewed.reshape(blocks.shape)


def solution(mesh):
    sizes = tuple(mesh.shape[name] for name in AXES)
    return jax.shard_map(
        functools.partial(on_device, sizes),
        mesh=mesh,
        in_specs=(P("gx", "gy", "gz", None, None, None), P()),
        out_specs=P("gx", "gy", "gz", None, None, None),
        check_vma=False,
    )
```

```python
import functools

import jax
import jax.numpy as jnp
from jax import lax
from jax.experimental import pallas as pl
from jax.experimental.pallas import tpu as pltpu
from jax.sharding import PartitionSpec as P

MESH = pl.DeviceIdType.MESH
AXES = ("gx", "gy", "gz")


def directions(sizes):
    found = []
    for axis, size in enumerate(sizes):
        if size == 2:
            found.append((axis, 0))
        elif size > 2:
            found.extend([(axis, -1), (axis, 1)])
    return found


def split(value):
    head = value.astype(jnp.bfloat16)
    tail = (value - head.astype(jnp.float32)).astype(jnp.bfloat16)
    return jnp.concatenate([head, tail], axis=1)


def product(left, right):
    width = right.shape[1] // 2
    both = jnp.dot(left, jnp.concatenate([right, right], axis=0), preferred_element_type=jnp.float32)
    return both[:, :width] + both[:, width:]


def kernel(
    sizes, cols_there, blocks, out,
    cols, own, far_diag, far_edge, edge, half, acc, res,
    cols_sem, load_sem, send_d, recv_d, send_e, recv_e, ready,
):
    dirs = directions(sizes)
    count = len(dirs)
    kslots, block_size = own.shape[0], own.shape[1]
    where_am_i = [lax.axis_index(name) for name in AXES]
    strides = (sizes[1] * sizes[2], sizes[2], 1)
    me = sum(place * stride for place, stride in zip(where_am_i, strides))

    def opposite(d):
        axis, step = dirs[d]
        return dirs.index((axis, -step))

    def target(d):
        axis, step = dirs[d]
        place = where_am_i[axis]
        return (1 - place) if step == 0 else place + step

    def neighbour_id(d):
        axis, _ = dirs[d]
        return me + (target(d) - where_am_i[axis]) * strides[axis]

    def exists(d):
        axis, step = dirs[d]
        if step == 0:
            return None
        place = where_am_i[axis]
        return place > 0 if step < 0 else place < sizes[axis] - 1

    def if_exists(d, action):
        there = exists(d)
        if there is None:
            action()
        else:
            pl.when(there)(action)

    def send(d, src, dst, send_sem, recv_sem):
        return pltpu.make_async_remote_copy(
            src_ref=src,
            dst_ref=dst.at[opposite(d)],
            send_sem=send_sem.at[d],
            recv_sem=recv_sem.at[opposite(d)],
            device_id={AXES[dirs[d][0]]: target(d)},
            device_id_type=MESH,
        )

    def arrival(d, src, dst, send_sem, recv_sem):
        return pltpu.make_async_remote_copy(
            src_ref=src,
            dst_ref=dst.at[d],
            send_sem=send_sem.at[d],
            recv_sem=recv_sem.at[d],
            device_id={AXES[dirs[d][0]]: target(d)},
            device_id_type=MESH,
        )

    def greeted(d):
        axis, step = dirs[d]
        place = where_am_i[axis]
        if step == 0:
            return place == 1
        low = place + (step - 1) // 2
        greeter_is_low = low % 2 == 1 if axis == 2 else True
        return greeter_is_low if step < 0 else jnp.logical_not(greeter_is_low)

    def answering(d):
        there, by = exists(d), greeted(d)
        return by if there is None else jnp.logical_and(there, by)

    def greeting(d):
        there, by = exists(d), jnp.logical_not(greeted(d))
        return by if there is None else jnp.logical_and(there, by)

    lowers = [d for d in range(count) if dirs[d][1] <= 0 or dirs[d][0] == 2]
    uppers = [d for d in range(count) if dirs[d][1] >= 0 or dirs[d][0] == 2]

    def send_diag(d):
        return send(d, blocks.at[0], far_diag, send_d, recv_d)

    def send_edge(d):
        return send(d, edge.at[d], far_edge, send_e, recv_e)

    barrier = pltpu.get_barrier_semaphore()
    for d in uppers:

        @pl.when(greeting(d))
        def _(d=d):
            pl.semaphore_signal(
                barrier, inc=1, device_id={AXES[dirs[d][0]]: target(d)}, device_id_type=MESH
            )

    named_load = pltpu.make_async_copy(cols_there, cols, cols_sem)
    named_load.start()
    peers = jnp.int32(0)
    for d in lowers:
        peers = peers + answering(d).astype(jnp.int32)

    @pl.when(peers > 0)
    def _():
        pl.semaphore_wait(barrier, peers)

    for d in lowers:

        @pl.when(answering(d))
        def _(d=d):
            pl.semaphore_signal(
                ready.at[opposite(d)], inc=1, device_id={AXES[dirs[d][0]]: target(d)}, device_id_type=MESH
            )
            send_diag(d).start()

    load = pltpu.make_async_copy(blocks, own, load_sem)
    load.start()
    for d in range(count):
        there = exists(d)
        if there is not None:

            @pl.when(jnp.logical_not(there))
            def _(d=d):
                far_diag[d] = jnp.zeros((block_size, block_size), jnp.float32)
                far_edge[d] = jnp.zeros((block_size, block_size), jnp.float32)

    named_load.wait()
    named = [cols[where_am_i[0], where_am_i[1], where_am_i[2], s] for s in range(kslots)]
    matches = [[named[s] == neighbour_id(d) for s in range(1, kslots)] for d in range(count)]
    load.wait()
    for d in range(count):
        total = jnp.where(matches[d][0], own[1], 0.0)
        for s in range(2, kslots):
            total = total + jnp.where(matches[d][s - 1], own[s], 0.0)
        edge[d] = total
    for d in lowers:
        pl.when(answering(d))(lambda d=d: send_edge(d).start())
    for d in uppers:

        @pl.when(greeting(d))
        def _(d=d):
            pl.semaphore_wait(ready.at[d], 1)
            send_diag(d).start()
            send_edge(d).start()

    half[0] = split(own[0])
    for d in range(count):
        half[1 + d] = split(edge[d])
    for d in range(count):
        acc[d] = product(half[0], half[1 + d])
    square = product(half[0], half[0])
    late = [d for d in range(count) if dirs[d][0] < 2]
    early = [d for d in range(count) if dirs[d][0] == 2]
    for group in (early, late):
        for d in group:
            if_exists(d, lambda d=d: arrival(d, blocks.at[0], far_diag, send_d, recv_d).wait_recv())
        arrived = {d: split(far_diag[d]) for d in group}
        near = {d: acc[d] + product(half[1 + d], arrived[d]) for d in group}
        for d in group:
            repeats = sum(match.astype(jnp.int32) for match in matches[d]).astype(jnp.float32)
            weighted = split(near[d] * repeats)
            half[1 + count + d] = weighted
            acc[d] = 3.0 * near[d] - 2.0 * product(weighted, arrived[d])
    cubed = jnp.zeros((block_size, block_size), jnp.float32)
    for group in (early, late):
        for d in group:
            if_exists(d, lambda d=d: arrival(d, edge.at[d], far_edge, send_e, recv_e).wait_recv())
        for d in group:
            both = product(
                jnp.concatenate([half[1 + d], half[1 + count + d]], axis=0), split(far_edge[d])
            )
            square = square + both[:block_size]
            cubed = cubed + both[block_size:]
    own_square = split(square)
    for d in range(count):
        res[1 + d] = acc[d] - 2.0 * product(own_square, half[1 + d])
    cubed = cubed + product(own_square, half[0])
    res[0] = jnp.zeros((block_size, block_size), jnp.float32)
    out[0] = 3.0 * square - 2.0 * cubed
    for s in range(1, kslots):
        index = jnp.int32(0)
        for d in range(count):
            index = jnp.where(matches[d][s - 1], 1 + d, index)
        out[s] = res[index]
    for d in range(count):
        if_exists(d, lambda d=d: send_edge(d).wait_send())
        if_exists(d, lambda d=d: send_diag(d).wait_send())


def on_device(sizes, blocks, columns):
    kslots, block_size = blocks.shape[3], blocks.shape[4]
    count = len(directions(sizes))
    block = (block_size, block_size)
    renewed = pl.pallas_call(
        functools.partial(kernel, sizes),
        out_shape=pltpu.VMEM((kslots,) + block, jnp.float32),
        in_specs=[
            pl.BlockSpec(memory_space=pl.ANY),
            pl.BlockSpec(memory_space=pl.ANY),
        ],
        out_specs=pl.BlockSpec(memory_space=pltpu.VMEM),
        scratch_shapes=[
            pltpu.SMEM(columns.shape, jnp.int32),
            pltpu.VMEM((kslots,) + block, jnp.float32),
            pltpu.VMEM((count,) + block, jnp.float32),
            pltpu.VMEM((count,) + block, jnp.float32),
            pltpu.VMEM((count,) + block, jnp.float32),
            pltpu.VMEM((1 + 2 * count, block_size, 2 * block_size), jnp.bfloat16),
            pltpu.VMEM((count,) + block, jnp.float32),
            pltpu.VMEM((1 + count,) + block, jnp.float32),
            pltpu.SemaphoreType.DMA,
            pltpu.SemaphoreType.DMA,
            pltpu.SemaphoreType.DMA((count,)),
            pltpu.SemaphoreType.DMA((count,)),
            pltpu.SemaphoreType.DMA((count,)),
            pltpu.SemaphoreType.DMA((count,)),
            pltpu.SemaphoreType.REGULAR((count,)),
        ],
        compiler_params=pltpu.CompilerParams(
            collective_id=0, has_side_effects=True
        ),
    )(columns, blocks.reshape((kslots,) + block))
    return renewed.reshape(blocks.shape)


def solution(mesh):
    sizes = tuple(mesh.shape[name] for name in AXES)
    return jax.shard_map(
        functools.partial(on_device, sizes),
        mesh=mesh,
        in_specs=(P("gx", "gy", "gz", None, None, None), P()),
        out_specs=P("gx", "gy", "gz", None, None, None),
        check_vma=False,
    )
```

```python
import functools

import jax
import jax.numpy as jnp
from jax import lax
from jax.experimental import pallas as pl
from jax.experimental.pallas import tpu as pltpu
from jax.sharding import PartitionSpec as P

MESH = pl.DeviceIdType.MESH
AXES = ("gx", "gy", "gz")


def directions(sizes):
    found = []
    for axis, size in enumerate(sizes):
        if size == 2:
            found.append((axis, 0))
        elif size > 2:
            found.extend([(axis, -1), (axis, 1)])
    return found


def split(value):
    head = value.astype(jnp.bfloat16)
    tail = (value - head.astype(jnp.float32)).astype(jnp.bfloat16)
    return jnp.concatenate([head, tail], axis=1)


def product(left, right):
    width = right.shape[1] // 2
    both = jnp.dot(left, jnp.concatenate([right, right], axis=0), preferred_element_type=jnp.float32)
    return both[:, :width] + both[:, width:]


def kernel(
    sizes, cols_there, blocks, out,
    cols, own, far_diag, far_edge, edge, half, acc, res,
    cols_sem, load_sem, send_d, recv_d, send_e, recv_e, ready,
):
    dirs = directions(sizes)
    count = len(dirs)
    kslots, block_size = own.shape[0], own.shape[1]
    where_am_i = [lax.axis_index(name) for name in AXES]
    strides = (sizes[1] * sizes[2], sizes[2], 1)
    me = sum(place * stride for place, stride in zip(where_am_i, strides))

    def opposite(d):
        axis, step = dirs[d]
        return dirs.index((axis, -step))

    def target(d):
        axis, step = dirs[d]
        place = where_am_i[axis]
        return (1 - place) if step == 0 else place + step

    def neighbour_id(d):
        axis, _ = dirs[d]
        return me + (target(d) - where_am_i[axis]) * strides[axis]

    def exists(d):
        axis, step = dirs[d]
        if step == 0:
            return None
        place = where_am_i[axis]
        return place > 0 if step < 0 else place < sizes[axis] - 1

    def if_exists(d, action):
        there = exists(d)
        if there is None:
            action()
        else:
            pl.when(there)(action)

    def send(d, src, dst, send_sem, recv_sem):
        return pltpu.make_async_remote_copy(
            src_ref=src,
            dst_ref=dst.at[opposite(d)],
            send_sem=send_sem.at[d],
            recv_sem=recv_sem.at[opposite(d)],
            device_id={AXES[dirs[d][0]]: target(d)},
            device_id_type=MESH,
        )

    def arrival(d, src, dst, send_sem, recv_sem):
        return pltpu.make_async_remote_copy(
            src_ref=src,
            dst_ref=dst.at[d],
            send_sem=send_sem.at[d],
            recv_sem=recv_sem.at[d],
            device_id={AXES[dirs[d][0]]: target(d)},
            device_id_type=MESH,
        )

    def greeted(d):
        axis, step = dirs[d]
        place = where_am_i[axis]
        if step == 0:
            return place == 1
        low = place + (step - 1) // 2
        greeter_is_low = low % 2 == 1 if axis == 2 else True
        return greeter_is_low if step < 0 else jnp.logical_not(greeter_is_low)

    def answering(d):
        there, by = exists(d), greeted(d)
        return by if there is None else jnp.logical_and(there, by)

    def greeting(d):
        there, by = exists(d), jnp.logical_not(greeted(d))
        return by if there is None else jnp.logical_and(there, by)

    lowers = [d for d in range(count) if dirs[d][1] <= 0 or dirs[d][0] == 2]
    uppers = [d for d in range(count) if dirs[d][1] >= 0 or dirs[d][0] == 2]

    def send_diag(d):
        return send(d, blocks.at[0], far_diag, send_d, recv_d)

    def send_edge(d):
        return send(d, edge.at[d], far_edge, send_e, recv_e)

    barrier = pltpu.get_barrier_semaphore()
    for d in uppers:

        @pl.when(greeting(d))
        def _(d=d):
            pl.semaphore_signal(
                barrier, inc=1, device_id={AXES[dirs[d][0]]: target(d)}, device_id_type=MESH
            )

    named_load = pltpu.make_async_copy(cols_there, cols, cols_sem)
    named_load.start()
    peers = jnp.int32(0)
    for d in lowers:
        peers = peers + answering(d).astype(jnp.int32)

    @pl.when(peers > 0)
    def _():
        pl.semaphore_wait(barrier, peers)

    for d in lowers:

        @pl.when(answering(d))
        def _(d=d):
            pl.semaphore_signal(
                ready.at[opposite(d)], inc=1, device_id={AXES[dirs[d][0]]: target(d)}, device_id_type=MESH
            )
            send_diag(d).start()

    load = pltpu.make_async_copy(blocks, own, load_sem)
    load.start()
    for d in range(count):
        there = exists(d)
        if there is not None:

            @pl.when(jnp.logical_not(there))
            def _(d=d):
                far_diag[d] = jnp.zeros((block_size, block_size), jnp.float32)
                far_edge[d] = jnp.zeros((block_size, block_size), jnp.float32)

    named_load.wait()
    named = [cols[where_am_i[0], where_am_i[1], where_am_i[2], s] for s in range(kslots)]
    matches = [[named[s] == neighbour_id(d) for s in range(1, kslots)] for d in range(count)]
    load.wait()
    for d in range(count):
        total = jnp.where(matches[d][0], own[1], 0.0)
        for s in range(2, kslots):
            total = total + jnp.where(matches[d][s - 1], own[s], 0.0)
        edge[d] = total
    for d in lowers:
        pl.when(answering(d))(lambda d=d: send_edge(d).start())
    for d in uppers:

        @pl.when(greeting(d))
        def _(d=d):
            pl.semaphore_wait(ready.at[d], 1)
            send_diag(d).start()
            send_edge(d).start()

    half[0] = split(own[0])
    for d in range(count):
        half[1 + d] = split(edge[d])
    for d in range(count):
        acc[d] = product(half[0], half[1 + d])
    square = product(half[0], half[0])
    late = [d for d in range(count) if dirs[d][0] < 2]
    early = [d for d in range(count) if dirs[d][0] == 2]
    for group in (early, late):
        for d in group:
            if_exists(d, lambda d=d: arrival(d, blocks.at[0], far_diag, send_d, recv_d).wait_recv())
        arrived = {d: split(far_diag[d]) for d in group}
        near = {d: acc[d] + product(half[1 + d], arrived[d]) for d in group}
        for d in group:
            repeats = sum(match.astype(jnp.int32) for match in matches[d]).astype(jnp.float32)
            weighted = split(near[d] * repeats)
            half[1 + count + d] = weighted
            acc[d] = 3.0 * near[d] - 2.0 * product(weighted, arrived[d])
    cubed = jnp.zeros((block_size, block_size), jnp.float32)
    for group in (early, late):
        for d in group:
            if_exists(d, lambda d=d: arrival(d, edge.at[d], far_edge, send_e, recv_e).wait_recv())
        for d in group:
            half[1 + 2 * count + d] = split(far_edge[d])
            square = square + product(half[1 + d], half[1 + 2 * count + d])
        if group is early:
            for d in group:
                cubed = cubed + product(half[1 + count + d], half[1 + 2 * count + d])
    own_square = split(square)
    for d in late:
        cubed = cubed + product(half[1 + count + d], half[1 + 2 * count + d])
    wide = jnp.concatenate([half[d] for d in range(1 + count)], axis=1)
    wide = jnp.dot(
        own_square, jnp.concatenate([wide, wide], axis=0), preferred_element_type=jnp.float32
    )
    for d in range(count):
        at = 2 * block_size * (1 + d)
        res[1 + d] = acc[d] - 2.0 * (
            wide[:, at : at + block_size] + wide[:, at + block_size : at + 2 * block_size]
        )
    cubed = cubed + (wide[:, :block_size] + wide[:, block_size : 2 * block_size])
    res[0] = jnp.zeros((block_size, block_size), jnp.float32)
    out[0] = 3.0 * square - 2.0 * cubed
    for s in range(1, kslots):
        index = jnp.int32(0)
        for d in range(count):
            index = jnp.where(matches[d][s - 1], 1 + d, index)
        out[s] = res[index]
    for d in range(count):
        if_exists(d, lambda d=d: send_edge(d).wait_send())
        if_exists(d, lambda d=d: send_diag(d).wait_send())


def on_device(sizes, blocks, columns):
    kslots, block_size = blocks.shape[3], blocks.shape[4]
    count = len(directions(sizes))
    block = (block_size, block_size)
    renewed = pl.pallas_call(
        functools.partial(kernel, sizes),
        out_shape=pltpu.VMEM((kslots,) + block, jnp.float32),
        in_specs=[
            pl.BlockSpec(memory_space=pl.ANY),
            pl.BlockSpec(memory_space=pl.ANY),
        ],
        out_specs=pl.BlockSpec(memory_space=pltpu.VMEM),
        scratch_shapes=[
            pltpu.SMEM(columns.shape, jnp.int32),
            pltpu.VMEM((kslots,) + block, jnp.float32),
            pltpu.VMEM((count,) + block, jnp.float32),
            pltpu.VMEM((count,) + block, jnp.float32),
            pltpu.VMEM((count,) + block, jnp.float32),
            pltpu.VMEM((1 + 3 * count, block_size, 2 * block_size), jnp.bfloat16),
            pltpu.VMEM((count,) + block, jnp.float32),
            pltpu.VMEM((1 + count,) + block, jnp.float32),
            pltpu.SemaphoreType.DMA,
            pltpu.SemaphoreType.DMA,
            pltpu.SemaphoreType.DMA((count,)),
            pltpu.SemaphoreType.DMA((count,)),
            pltpu.SemaphoreType.DMA((count,)),
            pltpu.SemaphoreType.DMA((count,)),
            pltpu.SemaphoreType.REGULAR((count,)),
        ],
        compiler_params=pltpu.CompilerParams(
            collective_id=0, has_side_effects=True
        ),
    )(columns, blocks.reshape((kslots,) + block))
    return renewed.reshape(blocks.shape)


def solution(mesh):
    sizes = tuple(mesh.shape[name] for name in AXES)
    return jax.shard_map(
        functools.partial(on_device, sizes),
        mesh=mesh,
        in_specs=(P("gx", "gy", "gz", None, None, None), P()),
        out_specs=P("gx", "gy", "gz", None, None, None),
        check_vma=False,
    )
```
